32 devices in a mesh: groups: 2 (over y), expert: 4 (over z), dp: 2 (over x), inner: 2 (over core).
Axes of the slice: x: 2, y: 2, z: 4, core: 2. Of those that a mesh axis runs over, the one named last changes fastest.
Arguments:
- tokens: bfloat16 [2048, 1536], P(('groups', 'expert', 'dp'), 'inner'), parts along dimension 0, may hold values from -6 to 6
- out_grad: bfloat16 [2048, 1536], P(('groups', 'expert', 'dp'), 'inner'), parts along dimension 0, may hold values from -6 to 6
- expert_ids: int32 [2048, 8], P(('groups', 'expert', 'dp')), parts along dimension 0, may hold values from 0 to 63, all different within a row; in each aligned block of 128 rows (0 to 127, 128 to 255, ...) at most 17 rows name the same one
- gate_probs: float32 [2048, 8], P(('groups', 'expert', 'dp')), parts along dimension 0, may hold values from 0.05 to 0.5
- gate_weight: bfloat16 [64, 1536, 384], P('expert', 'inner', 'dp'), may hold values from -0.15625 to 0.15625
- up_weight: bfloat16 [64, 1536, 384], P('expert', 'inner', 'dp'), may hold values from -0.15625 to 0.15625
- down_weight: bfloat16 [64, 384, 1536], P('expert', 'dp', 'inner'), may hold values from -0.3125 to 0.3125
Outputs:
- token_grad: bfloat16 [2048, 1536], P(('groups', 'expert', 'dp'), 'inner'), parts along dimension 0
- prob_grad: float32 [2048, 8], P(('groups', 'expert', 'dp')), parts along dimension 0
- gate_weight_grad: bfloat16 [128, 1536, 384], P(('groups', 'expert'), 'inner', 'dp'), parts along dimension 0
- up_weight_grad: bfloat16 [128, 1536, 384], P(('groups', 'expert'), 'inner', 'dp'), parts along dimension 0
- down_weight_grad: bfloat16 [128, 384, 1536], P(('groups', 'expert'), 'dp', 'inner'), parts along dimension 0
The draws below stay inside these ranges and needn't reach their ends.
There are 2 independent parts, one for each index of `groups`. The reference program is written for one: setup_inputs(seed, part) draws one part's arguments, and reference() takes and returns one part's arrays. A program takes and returns all parts, laid end to end along the dimension named above; an argument that names none is the same for every part. Nothing has to cross between parts.
Inputs may be any that keep to these rules, and one draw needn't show every extreme that they name: `expert_ids`: within the rows of one block of 128 tokens no expert is chosen more than 17 times, and some expert is chosen exactly 17 times in some block; a token's 8 experts differ.
All inputs are finite; a program needn't handle non-finite values.
Results may differ from the reference program's by a relative error of at most 0.015.
Values may be sent and summed in bfloat16 or wider, within the bound.
A program may use at most 192 MiB of HBM per device.

```python
import math
import jax
import jax.numpy as jnp
import numpy as np
from jax import lax

D = 1536
FF = 384
TOPK = 8
TOK_DEV = 128
E = 64
CAP = 17
TOKENS = 1024
N_EXPERT = 4
N_DP = 2
N_INNER = 2


def levels(stream_key, shape, pieces, least, high):
    def one(axis_at, blocks):
        heights = jax.random.uniform(jax.random.fold_in(jax.random.fold_in(stream_key, 6), axis_at), (blocks,), jnp.float32, least / len(pieces), high / len(pieces))
        return jnp.repeat(jnp.exp(heights), shape[axis_at] // blocks).reshape((-1,) + (1,) * (len(shape) - axis_at - 1))

    factor_of = one(*pieces[0])
    for cut in pieces[1:]:
        factor_of = factor_of * one(*cut)
    return factor_of


def shared_out(key, own, number, rows, count, top, reach, slope):
    order = jax.random.permutation(key, count)
    heavy_load, common = portions_of(count, rows * top, reach, slope, True), portions_of(count, rows * top, reach, slope, False)
    places = jnp.arange(count)

    def named(sizes, rotation):
        used = int((sizes > 0).sum())
        fixed = max(1, used // 4)
        passed = fixed + (places - fixed + rotation * (used - fixed)) % max(1, count - fixed)
        return jnp.zeros((count,), jnp.int32).at[order[jnp.where(places < fixed, places, passed)]].set(jnp.asarray(sizes, jnp.int32))

    sizes = jnp.where(number % 4 == 0, named(heavy_load, number // 4), named(common, number - number // 4 - 1))
    mixed = jax.random.permutation(jax.random.fold_in(own, 3), count)
    giver, taker = mixed[0:count // 2 * 2:2], mixed[1:count // 2 * 2:2]
    slack = jnp.minimum(sizes[giver] - 1, reach - sizes[taker]) // 2
    slack = jnp.where((giver == order[0]) | (taker == order[0]) | (sizes[taker] == 0), 0, jnp.maximum(slack, 0))
    passed = jax.random.randint(jax.random.fold_in(own, 4), (count // 2,), 0, 1 << 20) % (slack + 1)
    sizes = sizes.at[giver].add(-passed).at[taker].add(passed)
    members = jnp.searchsorted(jnp.cumsum(sizes), jnp.arange(rows * top), side="right").astype(jnp.int32)
    listing = members.reshape(top, rows).T
    listing = listing[jax.random.permutation(jax.random.fold_in(own, 1), rows)]
    rotation = jax.random.randint(jax.random.fold_in(own, 2), (rows, 1), 0, top)
    return jnp.take_along_axis(listing, (jnp.arange(top)[None, :] + rotation) % top, axis=1)


def portions_of(number_of, total, reach, skew, full):
    weights = [(1 << 20) // math.isqrt(standing ** skew) + 1 for standing in range(1, number_of + 1)]
    largest = reach if full else min(reach, max(-(-total // number_of), total * weights[0] // sum(weights)))
    least = 1 if total - largest >= number_of - 1 else 0
    counts, surplus = [largest] + [least] * (number_of - 1), total - largest - least * (number_of - 1)
    while surplus > 0:
        movable = [i for i in range(1, number_of) if counts[i] < largest] or [i for i in range(1, number_of) if counts[i] < reach]
        mass, left = sum([weights[i] for i in movable]), surplus
        for i in movable:
            extra = min(reach - counts[i], max(1, left * weights[i] // mass), surplus)
            counts[i] = counts[i] + extra
            surplus = surplus - extra
    return np.array(counts)


def scatter_about(stream_key, shape, width, limit, split=(), kind=jnp.bfloat16):
    gain = levels(stream_key, shape, split, -0.22, 0.18) if split else 1.0
    result = jax.random.normal(stream_key, shape, jnp.float32) * width * gain
    return jnp.minimum(jnp.maximum(result, -limit), limit).astype(kind)


def setup_inputs(seed: int = 0, part: int = 0) -> dict:
    splits = jax.random.split(jax.random.key(seed), 8)
    part_splits = jax.random.split(jax.random.fold_in(splits[7], part), 8)
    tokens = scatter_about(part_splits[0], (TOKENS, D), 1.0, 6.0, ((0, 8), (1, 2)))
    out_grad = scatter_about(part_splits[1], (TOKENS, D), 1.0, 6.0, ((0, 8), (1, 2)))
    expert_ids_keys = jax.random.split(jax.random.fold_in(part_splits[2], 1), TOKENS // TOK_DEV)
    expert_ids_turns = jax.random.permutation(jax.random.fold_in(part_splits[2], 3), TOKENS // TOK_DEV)
    expert_ids = jax.vmap(lambda own, number: shared_out(jax.random.fold_in(part_splits[2], 2), own, number, TOK_DEV, E, TOPK, CAP, 1))(expert_ids_keys, expert_ids_turns).reshape((TOKENS, TOPK))
    gate_probs = jnp.clip(jnp.exp(math.log(0.5) - 2.3025851 * jax.random.uniform(part_splits[3], (TOKENS, TOPK), jnp.float32) ** levels(part_splits[3], (TOKENS, TOPK), ((0, 8),), -0.2, 0.2)), 0.05, 0.5)
    gate_weight = scatter_about(splits[4], (E, D, FF), D ** -0.5, 0.15625, ((0, 4), (1, 2), (2, 2)))
    up_weight = scatter_about(splits[5], (E, D, FF), D ** -0.5, 0.15625, ((0, 4), (1, 2), (2, 2)))
    down_weight = scatter_about(splits[6], (E, FF, D), FF ** -0.5, 0.3125, ((0, 4), (1, 2), (2, 2)))
    return dict(tokens=tokens, out_grad=out_grad, expert_ids=expert_ids, gate_probs=gate_probs, gate_weight=gate_weight, up_weight=up_weight, down_weight=down_weight)


def rounded(value):
    return lax.optimization_barrier(value.astype(jnp.bfloat16)).astype(jnp.float32)


def reference(tokens, out_grad, expert_ids, gate_probs, gate_weight, up_weight, down_weight):
    blocks = N_EXPERT * N_DP
    pair_count = TOK_DEV * TOPK
    half_width = D // N_INNER
    row_count = N_EXPERT * CAP
    chosen = expert_ids.reshape(blocks, pair_count).astype(jnp.int32)
    expert_range = jnp.arange(E, dtype=jnp.int32)
    matches = (chosen[:, :, None] == expert_range[None, None, :]).astype(jnp.int32)
    before = jnp.cumsum(matches, axis=1) - matches
    slot_index = jnp.sum(before * matches, axis=2).astype(jnp.int32)
    table_pos = chosen * CAP + slot_index
    block_ids = jnp.broadcast_to(jnp.arange(blocks, dtype=jnp.int32)[:, None], (blocks, pair_count))
    pair_ids = jnp.arange(blocks * pair_count, dtype=jnp.int32).reshape(blocks, pair_count)
    table = jnp.zeros((blocks, E * CAP), jnp.int32).at[block_ids, table_pos].set(pair_ids)
    present = jnp.zeros((blocks, E * CAP), jnp.float32).at[block_ids, table_pos].set(1.0)
    table = table.reshape(N_EXPERT, N_DP, E, CAP).transpose(2, 1, 0, 3).reshape(E, N_DP, row_count)
    present = present.reshape(N_EXPERT, N_DP, E, CAP).transpose(2, 1, 0, 3).reshape(E, N_DP, row_count)
    prob_flat = rounded(gate_probs.reshape(-1).astype(jnp.float32))

    def per_expert(carry, expert):
        grad_acc, prob_acc = carry
        pair_e = table[expert]
        here_e = present[expert]
        token_e = pair_e // TOPK
        rows_in = tokens[token_e].astype(jnp.float32) * here_e[..., None]
        grads_in = out_grad[token_e].astype(jnp.float32) * here_e[..., None]
        probs_in = prob_flat[pair_e] * here_e
        wgate = gate_weight[expert].astype(jnp.float32)
        wup = up_weight[expert].astype(jnp.float32)
        wdown = down_weight[expert].astype(jnp.float32)
        split_rows = rows_in.reshape(N_DP, row_count, N_INNER, half_width)
        split_grads = grads_in.reshape(N_DP, row_count, N_INNER, half_width)
        gate_sum = jnp.sum(rounded(jnp.einsum("jrid,idf->ijrf", split_rows, wgate.reshape(N_INNER, half_width, FF))), axis=0)
        up_sum = jnp.sum(rounded(jnp.einsum("jrid,idf->ijrf", split_rows, wup.reshape(N_INNER, half_width, FF))), axis=0)
        sigmoid_gate = jax.nn.sigmoid(gate_sum)
        activated = gate_sum * sigmoid_gate
        hidden = rounded(activated * up_sum)
        slope_sum = jnp.sum(rounded(jnp.einsum("jrid,fid->ijrf", split_grads, wdown.reshape(FF, N_INNER, half_width))), axis=0)
        scores = rounded(jnp.sum(hidden * slope_sum, axis=-1))
        hidden_grad = probs_in[..., None] * slope_sum
        gate_back = rounded(hidden_grad * up_sum * sigmoid_gate * (1.0 + gate_sum * (1.0 - sigmoid_gate)))
        up_back = rounded(hidden_grad * activated)
        row_grad = rounded(jnp.einsum("jrf,df->jrd", gate_back, wgate) + jnp.einsum("jrf,df->jrd", up_back, wup))
        grad_acc = grad_acc.at[token_e.reshape(-1)].add(row_grad.reshape(-1, D))
        prob_acc = prob_acc.at[pair_e.reshape(-1)].add(scores.reshape(-1))
        grad_gate = jnp.sum(rounded(jnp.einsum("jrd,jrf->jdf", rows_in, gate_back)), axis=0)
        grad_up = jnp.sum(rounded(jnp.einsum("jrd,jrf->jdf", rows_in, up_back)), axis=0)
        down_rows = rounded(probs_in[..., None] * grads_in)
        grad_down = jnp.sum(rounded(jnp.einsum("jrf,jrd->jfd", hidden, down_rows)), axis=0)
        outputs = (grad_gate.astype(jnp.bfloat16), grad_up.astype(jnp.bfloat16), grad_down.astype(jnp.bfloat16))
        return (grad_acc, prob_acc), outputs

    start = (jnp.zeros((TOKENS, D), jnp.float32), jnp.zeros((TOKENS * TOPK,), jnp.float32))
    finals, stacked = lax.scan(per_expert, start, jnp.arange(E, dtype=jnp.int32))
    grad_acc, prob_acc = finals
    return (grad_acc.astype(jnp.bfloat16), prob_acc.reshape(TOKENS, TOPK), stacked[0], stacked[1], stacked[2])
```

```python
import jax
import jax.numpy as jnp
from jax import lax
from jax.sharding import PartitionSpec as P

F32 = jnp.float32
BF16 = jnp.bfloat16


def select_rows(packed, width, top_count, per_dev, block_rows, capacity):
    total = packed.shape[0]
    blocks = total // block_rows
    run = 4 if blocks % 4 == 0 else 1
    runs = blocks // run
    span = run * block_rows
    rows = -(-run * capacity // 16) * 16
    ids = packed[:, 2 * width : 2 * width + top_count].astype(jnp.int32)
    probs = packed[:, 2 * width + top_count : 2 * width + 2 * top_count]
    mine = lax.axis_index("expert") * per_dev + jnp.arange(per_dev, dtype=jnp.int32)
    hits = ids[:, :, None] == mine[None, None, :]
    member = jnp.any(hits, axis=1).reshape(runs, span, per_dev)
    weight = jnp.sum(jnp.where(hits, probs[:, :, None].astype(F32), 0.0), axis=1)
    weight = weight.reshape(runs, span, per_dev)
    at = jnp.arange(span, dtype=jnp.int32)
    earlier = (at[:, None] > at[None, :]).astype(BF16)
    slot = jnp.einsum("ts,gse->get", earlier, member.astype(BF16), preferred_element_type=F32)
    slot = jnp.where(member.transpose(0, 2, 1), slot.astype(jnp.int32), -1)
    places = jnp.arange(rows, dtype=jnp.int32)
    picked = slot[:, :, None, :] == places[None, None, :, None]
    row_prob = jnp.sum(jnp.where(picked, weight.transpose(0, 2, 1)[:, :, None, :], 0.0), axis=3)
    return picked.astype(BF16), row_prob, hits, runs, span, rows


def on_device(tokens, out_grad, expert_ids, gate_probs, gate_weight, up_weight, down_weight):
    tok_rows, width = tokens.shape
    top_count = expert_ids.shape[1]
    per_dev = gate_weight.shape[0]
    experts = per_dev * lax.axis_size("expert")
    capacity = tok_rows * top_count // experts + 1
    packed = jnp.concatenate(
        [tokens, out_grad, expert_ids.astype(BF16), gate_probs.astype(BF16)], axis=1
    )
    packed = lax.all_gather(packed, ("expert", "dp"), axis=0, tiled=True)
    picked, row_prob, hits, runs, span, rows = select_rows(
        packed, width, top_count, per_dev, tok_rows, capacity
    )
    both = packed[:, : 2 * width].reshape(runs, span, 2 * width)
    sorted_rows = jnp.einsum("gest,gtd->egsd", picked, both, preferred_element_type=F32)
    sorted_rows = sorted_rows.astype(BF16).reshape(per_dev, runs * rows, 2 * width)
    expert_rows, expert_grads = sorted_rows[:, :, :width], sorted_rows[:, :, width:]
    prob_col = row_prob.transpose(1, 0, 2).reshape(per_dev, runs * rows, 1)
    hid = gate_weight.shape[2]
    parts = jnp.concatenate(
        [
            jnp.einsum("jrd,jdf->jrf", expert_rows, gate_weight, preferred_element_type=F32),
            jnp.einsum("jrd,jdf->jrf", expert_rows, up_weight, preferred_element_type=F32),
            jnp.einsum("jrd,jfd->jrf", expert_grads, down_weight, preferred_element_type=F32),
        ],
        axis=2,
    ).astype(BF16)
    sums = lax.psum(parts, "inner").astype(F32)
    gate, up, slope = sums[..., :hid], sums[..., hid : 2 * hid], sums[..., 2 * hid :]
    sig = jax.nn.sigmoid(gate)
    act = gate * sig
    hidden = (act * up).astype(BF16)
    scores = jnp.sum(hidden.astype(F32) * slope, axis=-1)
    hidden_grad = prob_col * slope
    gate_back = (hidden_grad * up * sig * (1.0 + gate * (1.0 - sig))).astype(BF16)
    up_back = (hidden_grad * act).astype(BF16)
    row_grads = jnp.einsum("jrf,jdf->jrd", gate_back, gate_weight, preferred_element_type=F32)
    row_grads = (
        row_grads + jnp.einsum("jrf,jdf->jrd", up_back, up_weight, preferred_element_type=F32)
    ).astype(BF16)
    token_part = jnp.einsum(
        "gest,egsd->gtd",
        picked,
        row_grads.reshape(per_dev, runs, rows, width),
        preferred_element_type=F32,
    ).reshape(runs * span, width)
    score_rows = scores.reshape(per_dev, runs, rows).transpose(1, 0, 2)
    score_part = jnp.sum(picked.astype(F32) * score_rows[..., None], axis=2)
    score_part = score_part.transpose(0, 2, 1).reshape(runs * span, 1, per_dev)
    score_part = jnp.sum(jnp.where(hits, score_part, 0.0), axis=2)
    returned = lax.psum_scatter(
        jnp.concatenate([token_part, score_part], axis=1).astype(BF16),
        ("expert", "dp"),
        scatter_dimension=0,
        tiled=True,
    )
    grad_gate = jnp.einsum("jrd,jrf->jdf", expert_rows, gate_back, preferred_element_type=F32)
    grad_up = jnp.einsum("jrd,jrf->jdf", expert_rows, up_back, preferred_element_type=F32)
    down_rows = (prob_col * expert_grads.astype(F32)).astype(BF16)
    grad_down = jnp.einsum("jrf,jrd->jfd", hidden, down_rows, preferred_element_type=F32)
    return (
        returned[:, :width],
        returned[:, width:].astype(F32),
        grad_gate.astype(BF16),
        grad_up.astype(BF16),
        grad_down.astype(BF16),
    )


def solution(mesh):
    placed = (
        P(("groups", "expert", "dp"), "inner"),
        P(("groups", "expert", "dp"), "inner"),
        P(("groups", "expert", "dp"), None),
        P(("groups", "expert", "dp"), None),
        P("expert", "inner", "dp"),
        P("expert", "inner", "dp"),
        P("expert", "dp", "inner"),
    )
    return jax.shard_map(
        on_device,
        mesh=mesh,
        in_specs=placed,
        out_specs=(
            P(("groups", "expert", "dp"), "inner"),
            P(("groups", "expert", "dp"), None),
            P(("groups", "expert"), "inner", "dp"),
            P(("groups", "expert"), "inner", "dp"),
            P(("groups", "expert"), "dp", "inner"),
        ),
        check_vma=False,
    )
```

```python
import functools

import jax
import jax.numpy as jnp
from jax import lax
from jax.experimental import pallas as pl
from jax.experimental.pallas import tpu as pltpu
from jax.sharding import PartitionSpec as P

F32 = jnp.float32
BF16 = jnp.bfloat16


def select_rows(packed, width, top_count, per_dev, block_rows, capacity):
    total = packed.shape[0]
    blocks = total // block_rows
    run = 4 if blocks % 4 == 0 else 1
    runs = blocks // run
    span = run * block_rows
    rows = -(-run * capacity // 16) * 16
    ids = packed[:, 2 * width : 2 * width + top_count].astype(jnp.int32)
    probs = packed[:, 2 * width + top_count : 2 * width + 2 * top_count]
    mine = lax.axis_index("expert") * per_dev + jnp.arange(per_dev, dtype=jnp.int32)
    hits = ids[:, :, None] == mine[None, None, :]
    member = jnp.any(hits, axis=1).reshape(runs, span, per_dev)
    weight = jnp.sum(jnp.where(hits, probs[:, :, None].astype(F32), 0.0), axis=1)
    weight = weight.reshape(runs, span, per_dev)
    at = jnp.arange(span, dtype=jnp.int32)
    earlier = (at[:, None] > at[None, :]).astype(BF16)
    slot = jnp.einsum("ts,gse->get", earlier, member.astype(BF16), preferred_element_type=F32)
    slot = jnp.where(member.transpose(0, 2, 1), slot.astype(jnp.int32), -1)
    places = jnp.arange(rows, dtype=jnp.int32)
    picked = slot[:, :, None, :] == places[None, None, :, None]
    row_prob = jnp.sum(jnp.where(picked, weight.transpose(0, 2, 1)[:, :, None, :], 0.0), axis=3)
    return picked.astype(BF16), row_prob, hits, runs, span, rows


def on_device_wide(tokens, out_grad, expert_ids, gate_probs, gate_weight, up_weight, down_weight):
    tok_rows, width = tokens.shape
    top_count = expert_ids.shape[1]
    per_dev = gate_weight.shape[0]
    experts = per_dev * lax.axis_size("expert")
    capacity = tok_rows * top_count // experts + 1
    packed = jnp.concatenate(
        [tokens, out_grad, expert_ids.astype(BF16), gate_probs.astype(BF16)], axis=1
    )
    packed = lax.all_gather(packed, ("expert", "dp"), axis=0, tiled=True)
    picked, row_prob, hits, runs, span, rows = select_rows(
        packed, width, top_count, per_dev, tok_rows, capacity
    )
    both = packed[:, : 2 * width].reshape(runs, span, 2 * width)
    sorted_rows = jnp.einsum("gest,gtd->egsd", picked, both, preferred_element_type=F32)
    sorted_rows = sorted_rows.astype(BF16).reshape(per_dev, runs * rows, 2 * width)
    expert_rows, expert_grads = sorted_rows[:, :, :width], sorted_rows[:, :, width:]
    prob_col = row_prob.transpose(1, 0, 2).reshape(per_dev, runs * rows, 1)
    hid = gate_weight.shape[2]
    parts = jnp.concatenate(
        [
            jnp.einsum("jrd,jdf->jrf", expert_rows, gate_weight, preferred_element_type=F32),
            jnp.einsum("jrd,jdf->jrf", expert_rows, up_weight, preferred_element_type=F32),
            jnp.einsum("jrd,jfd->jrf", expert_grads, down_weight, preferred_element_type=F32),
        ],
        axis=2,
    ).astype(BF16)
    sums = lax.psum(parts, "inner").astype(F32)
    gate, up, slope = sums[..., :hid], sums[..., hid : 2 * hid], sums[..., 2 * hid :]
    sig = jax.nn.sigmoid(gate)
    act = gate * sig
    hidden = (act * up).astype(BF16)
    scores = jnp.sum(hidden.astype(F32) * slope, axis=-1)
    hidden_grad = prob_col * slope
    gate_back = (hidden_grad * up * sig * (1.0 + gate * (1.0 - sig))).astype(BF16)
    up_back = (hidden_grad * act).astype(BF16)
    row_grads = jnp.einsum("jrf,jdf->jrd", gate_back, gate_weight, preferred_element_type=F32)
    row_grads = (
        row_grads + jnp.einsum("jrf,jdf->jrd", up_back, up_weight, preferred_element_type=F32)
    ).astype(BF16)
    token_part = jnp.einsum(
        "gest,egsd->gtd",
        picked,
        row_grads.reshape(per_dev, runs, rows, width),
        preferred_element_type=F32,
    ).reshape(runs * span, width)
    score_rows = scores.reshape(per_dev, runs, rows).transpose(1, 0, 2)
    score_part = jnp.sum(picked.astype(F32) * score_rows[..., None], axis=2)
    score_part = score_part.transpose(0, 2, 1).reshape(runs * span, 1, per_dev)
    score_part = jnp.sum(jnp.where(hits, score_part, 0.0), axis=2)
    returned = lax.psum_scatter(
        jnp.concatenate([token_part, score_part], axis=1).astype(BF16),
        ("expert", "dp"),
        scatter_dimension=0,
        tiled=True,
    )
    grad_gate = jnp.einsum("jrd,jrf->jdf", expert_rows, gate_back, preferred_element_type=F32)
    grad_up = jnp.einsum("jrd,jrf->jdf", expert_rows, up_back, preferred_element_type=F32)
    down_rows = (prob_col * expert_grads.astype(F32)).astype(BF16)
    grad_down = jnp.einsum("jrf,jrd->jfd", hidden, down_rows, preferred_element_type=F32)
    return (
        returned[:, :width],
        returned[:, width:].astype(F32),
        grad_gate.astype(BF16),
        grad_up.astype(BF16),
        grad_down.astype(BF16),
    )


MESH = pl.DeviceIdType.MESH
PAD = 16
TRANS_LHS = (((0,), (0,)), ((), ()))
TRANS_RHS = (((1,), (1,)), ((), ()))


def dot_t(a, b, dims):
    return lax.dot_general(a, b, dims, preferred_element_type=F32)


def route_kernel(
    owners, run, slots, top_count,
    tok_in, grad_in, gw_hbm, uw_hbm, dw_hbm,
    out, xs_hbm, dr_hbm, back_hbm,
    tok, grd, gw, uw, dw, xs, gs, onehot, prob, part, peer, pair, tp, rx, rz,
    w_sem, send_z, recv_z, send_x, recv_x, send_i, recv_i, o_sem,
    send_a, recv_a, send_b, recv_b,
):
    m = lax.axis_index("expert")
    j = lax.axis_index("dp")
    i = lax.axis_index("inner")
    blocks, tall, width = tok.shape
    rows_blk = tall - PAD
    per_dev, rows, _ = xs.shape
    hid = gw.shape[2]
    hid_pad = part.shape[2] // 3
    runs = blocks // run
    span = run * rows_blk
    x_dev, i_dev = {"dp": 1 - j}, {"inner": 1 - i}

    loads = [
        pltpu.make_async_copy(s, d, w_sem.at[n])
        for n, (s, d) in enumerate(((gw_hbm, gw), (uw_hbm, uw), (dw_hbm, dw)))
    ]
    for load in loads:
        load.start()

    barrier = pltpu.get_barrier_semaphore()
    pl.semaphore_signal(barrier, inc=1, device_id=x_dev, device_id_type=MESH)
    pl.semaphore_signal(barrier, inc=1, device_id=i_dev, device_id_type=MESH)
    for d in range(1, owners):
        pl.semaphore_signal(
            barrier, inc=1, device_id={"expert": lax.rem(m + d, owners)}, device_id_type=MESH
        )
    pl.semaphore_wait(barrier, owners + 1)

    bufs = (tok, grd)
    own = (tok_in, grad_in)

    def hop(c, origin, right, step):
        block = 2 * origin + j
        lane = 0 if right else 1
        return pltpu.make_async_remote_copy(
            src_ref=own[c] if step == 0 else bufs[c].at[block],
            dst_ref=bufs[c].at[block],
            send_sem=send_z.at[c, lane, step],
            recv_sem=recv_z.at[c, lane, step],
            device_id={"expert": jnp.clip(m + 1 if right else m - 1, 0, owners - 1)},
            device_id_type=MESH,
        )

    def cross(c, origin, block_j, mine):
        return pltpu.make_async_remote_copy(
            src_ref=own[c] if mine else bufs[c].at[2 * origin + block_j],
            dst_ref=bufs[c].at[2 * origin + block_j],
            send_sem=send_x.at[c, origin],
            recv_sem=recv_x.at[c, origin],
            device_id=x_dev,
            device_id_type=MESH,
        )

    def can_send(right, origin):
        if right:
            return (m + 1 < owners) & (origin >= 0)
        return (m >= 1) & (origin < owners)

    for c in range(2):
        cross(c, m, j, True).start()
        for right in (True, False):
            @pl.when(can_send(right, m))
            def _(c=c, right=right):
                hop(c, m, right, 0).start()
    tok[2 * m + j] = tok_in[...]
    grd[2 * m + j] = grad_in[...]
    for step in range(1, owners):
        for c in range(2):
            for right in (True, False):
                origin = m - step if right else m + step

                @pl.when((origin >= 0) & (origin < owners))
                def _(c=c, right=right, origin=origin, step=step):
                    hop(c, origin, right, step - 1).wait_recv()
                    if step < owners - 1:
                        @pl.when(can_send(right, origin))
                        def _():
                            hop(c, origin, right, step).start()
                    cross(c, origin, j, False).start()

    at = lax.broadcasted_iota(jnp.int32, (span, span), 0)
    to = lax.broadcasted_iota(jnp.int32, (span, span), 1)
    earlier = (at < to).astype(BF16)
    place = lax.broadcasted_iota(jnp.int32, (slots, span), 0)
    expert_of = lax.broadcasted_iota(jnp.int32, (per_dev, span), 0) + m * per_dev

    def ids_of(g):
        return jnp.concatenate(
            [tok[g * run + b, rows_blk:tall, :rows_blk].astype(F32) for b in range(run)], axis=1
        )

    for o in range(owners):
        cross(0, o, 1 - j, False).wait_recv()
    for g in range(runs):
        meta = ids_of(g)
        ids = meta.astype(jnp.int32)
        member = jnp.zeros((per_dev, span), F32)
        weight = jnp.zeros((per_dev, span), F32)
        for k in range(top_count):
            hit = expert_of == ids[k : k + 1, :]
            member = member + jnp.where(hit, 1.0, 0.0)
            weight = weight + jnp.where(hit, meta[top_count + k : top_count + k + 1, :], 0.0)
        slot = jnp.dot(member.astype(BF16), earlier, preferred_element_type=F32).astype(jnp.int32)
        slot = jnp.where(member > 0.5, slot, -1)
        for e in range(per_dev):
            hit = place == slot[e : e + 1, :]
            onehot[g, e] = jnp.where(hit, 1.0, 0.0).astype(BF16)
            prob[e, g * slots : (g + 1) * slots, :] = jnp.sum(
                jnp.where(hit, weight[e : e + 1, :], 0.0), axis=1, keepdims=True
            )

    batch = 4 if per_dev % 4 == 0 else 1

    def spread(buf, dest):
        for g in range(runs):
            whole = buf[g * run : (g + 1) * run, :rows_blk, :].reshape(span, width)

            @pl.loop(0, per_dev // batch)
            def _(n):
                pick = onehot[g, pl.ds(n * batch, batch)].reshape(batch * slots, span)
                got = jnp.dot(pick, whole, preferred_element_type=F32).astype(BF16)
                dest[pl.ds(n * batch, batch), g * slots : (g + 1) * slots, :] = got.reshape(
                    batch, slots, width
                )

    spread(tok, xs)
    for load in loads:
        load.wait()
    xs_out = pltpu.make_async_copy(xs, xs_hbm, o_sem.at[2, 0])
    xs_out.start()

    @pl.loop(0, per_dev)
    def _(e):
        rows_e = xs[e]
        part[e, :, 0:hid] = jnp.dot(rows_e, gw[e], preferred_element_type=F32).astype(BF16)
        part[e, :, hid_pad : hid_pad + hid] = jnp.dot(
            rows_e, uw[e], preferred_element_type=F32
        ).astype(BF16)

    for o in range(owners):
        cross(1, o, 1 - j, False).wait_recv()
    spread(grd, gs)

    def swap(e):
        return pltpu.make_async_remote_copy(
            src_ref=part.at[e], dst_ref=peer.at[e],
            send_sem=send_i.at[e], recv_sem=recv_i.at[e],
            device_id=i_dev, device_id_type=MESH,
        )

    @pl.loop(0, per_dev)
    def _(e):
        part[e, :, 2 * hid_pad : 2 * hid_pad + hid] = dot_t(gs[e], dw[e], TRANS_RHS).astype(BF16)
        swap(e).start()

    pair[...] = jnp.zeros_like(pair)

    def back_out(e):
        return pltpu.make_async_copy(part.at[e], back_hbm.at[e], o_sem.at[0, e])

    def rows_out(e):
        return pltpu.make_async_copy(gs.at[e], dr_hbm.at[e], o_sem.at[1, e])

    @pl.loop(0, per_dev)
    def _(e):
        swap(e).wait()

        def total(n):
            cols = slice(n * hid_pad, n * hid_pad + hid)
            return part[e, :, cols].astype(F32) + peer[e, :, cols].astype(F32)

        gate, up, slope = total(0), total(1), total(2)
        col = prob[e]
        sig = jax.nn.sigmoid(gate)
        act = gate * sig
        hidden = (act * up).astype(BF16)
        score = jnp.sum(hidden.astype(F32) * slope, axis=1, keepdims=True)
        hidden_grad = col * slope
        gate_back = (hidden_grad * up * sig * (1.0 + gate * (1.0 - sig))).astype(BF16)
        up_back = (hidden_grad * act).astype(BF16)
        part[e, :, 0:hid] = gate_back
        part[e, :, hid_pad : hid_pad + hid] = up_back
        part[e, :, 2 * hid_pad : 2 * hid_pad + hid] = hidden
        back_out(e).start()
        gs[e] = (col * gs[e].astype(F32)).astype(BF16)
        rows_out(e).start()
        peer[e] = (dot_t(gate_back, gw[e], TRANS_RHS) + dot_t(up_back, uw[e], TRANS_RHS)).astype(
            BF16
        )
        for g in range(runs):
            ids = ids_of(g)[:top_count, :].astype(jnp.int32)
            seen = jnp.sum(
                onehot[g, e].astype(F32) * score[g * slots : (g + 1) * slots, :],
                axis=0, keepdims=True,
            )
            pair[g] += jnp.where(ids == m * per_dev + e, seen, 0.0)

    def give(o):
        return pltpu.make_async_remote_copy(
            src_ref=tp.at[2 * o + 1 - j], dst_ref=rx.at[o],
            send_sem=send_a.at[o], recv_sem=recv_a.at[o],
            device_id=x_dev, device_id_type=MESH,
        )

    def deliver(o, slot_at):
        return pltpu.make_async_remote_copy(
            src_ref=tp.at[2 * o + j], dst_ref=rz.at[slot_at],
            send_sem=send_b.at[o], recv_sem=recv_b.at[slot_at],
            device_id={"expert": o}, device_id_type=MESH,
        )

    for g in range(runs):
        back = peer[:, g * slots : (g + 1) * slots, :].reshape(per_dev * slots, width)
        pick = onehot[g].reshape(per_dev * slots, span)
        for b in range(run):
            n = g * run + b
            cols = slice(b * rows_blk, (b + 1) * rows_blk)
            tp[n, 0:rows_blk, :] = dot_t(pick[:, cols], back, TRANS_LHS).astype(BF16)
            tp[n, rows_blk:tall, :] = jnp.zeros((PAD, width), BF16)
            tp[n, rows_blk:tall, 0:rows_blk] = jnp.concatenate(
                [pair[g, :, cols], jnp.zeros((PAD - top_count, rows_blk), F32)], axis=0
            ).astype(BF16)
            if n % 2 == 1:
                give(n // 2).start()

    for o in range(owners):
        give(o).wait_recv()

        @pl.when(o != m)
        def _(o=o):
            tp[2 * o + j] = (tp[2 * o + j].astype(F32) + rx[o].astype(F32)).astype(BF16)
            deliver(o, m).start()

    acc = tp[2 * m + j].astype(F32) + rx[m].astype(F32)
    out[...] = acc
    for o in range(owners):
        @pl.when(o != m)
        def _(o=o):
            deliver(o, o).wait_recv()
            out[...] += rz[o].astype(F32)

    for o in range(owners):
        give(o).wait_send()

        @pl.when(o != m)
        def _(o=o):
            deliver(o, o).wait_send()
        for c in range(2):
            cross(c, o, j, False).wait_send()
    for step in range(owners - 1):
        for c in range(2):
            for right in (True, False):
                origin = m - step if right else m + step

                @pl.when(can_send(right, origin))
                def _(c=c, right=right, origin=origin, step=step):
                    hop(c, origin, right, step).wait_send()
    xs_out.wait()

    @pl.loop(0, per_dev)
    def _(e):
        back_out(e).wait()
        rows_out(e).wait()


def weights_kernel(hid, hid_pad, xs, dr, back, gate_out, up_out, down_out):
    rows_e = xs[0]
    gate_out[0] = dot_t(rows_e, back[0, :, 0:hid], TRANS_LHS).astype(BF16)
    up_out[0] = dot_t(rows_e, back[0, :, hid_pad : hid_pad + hid], TRANS_LHS).astype(BF16)
    down_out[0] = dot_t(back[0, :, 2 * hid_pad : 2 * hid_pad + hid], dr[0], TRANS_LHS).astype(BF16)


def on_device(tokens, out_grad, expert_ids, gate_probs, gate_weight, up_weight, down_weight):
    args = (tokens, out_grad, expert_ids, gate_probs, gate_weight, up_weight, down_weight)
    tok_rows, width = tokens.shape
    top_count = expert_ids.shape[1]
    per_dev, _, hid = gate_weight.shape
    owners = lax.axis_size("expert")
    blocks = owners * lax.axis_size("dp")
    capacity = tok_rows * top_count // (per_dev * owners) + 1
    run = 4 if blocks % 4 == 0 else 2
    runs = blocks // run
    slots = -(-run * capacity // 16) * 16
    rows = runs * slots
    hid_pad = -(-hid // 128) * 128
    tall = tok_rows + PAD
    scratch = [
        ((blocks, tall, width), BF16),
        ((blocks, tok_rows, width), BF16),
        (gate_weight.shape, BF16),
        (up_weight.shape, BF16),
        (down_weight.shape, BF16),
        ((per_dev, rows, width), BF16),
        ((per_dev, rows, width), BF16),
        ((runs, per_dev, slots, run * tok_rows), BF16),
        ((per_dev, rows, 1), F32),
        ((per_dev, rows, 3 * hid_pad), BF16),
        ((per_dev, rows, width), BF16),
        ((runs, top_count, run * tok_rows), F32),
        ((blocks, tall, width), BF16),
        ((owners, tall, width), BF16),
        ((owners, tall, width), BF16),
    ]
    need = 0
    for shape, dtype in scratch:
        lanes = -(-shape[-1] // 128) * 128
        size = lanes * (2 if dtype == BF16 else 4)
        for n in shape[:-1]:
            size *= n
        need += size
    fits = need < 54 * 2**20 and lax.axis_size("dp") == 2 and lax.axis_size("inner") == 2
    fits = fits and tok_rows == 128 and top_count == 8 and 3 * hid_pad == width
    if not fits:
        return on_device_wide(*args)
    meta = jnp.concatenate([expert_ids.astype(BF16).T, gate_probs.astype(BF16).T], axis=0)
    tok_in = jnp.concatenate([tokens, jnp.pad(meta, ((0, 0), (0, width - tok_rows)))], axis=0)
    vmem = pl.BlockSpec(memory_space=pltpu.VMEM)
    hbm = pl.BlockSpec(memory_space=pl.ANY)
    dma = pltpu.SemaphoreType.DMA
    out, xs, dr, back = pl.pallas_call(
        functools.partial(route_kernel, owners, run, slots, top_count),
        out_shape=(
            jax.ShapeDtypeStruct((tall, width), F32),
            jax.ShapeDtypeStruct((per_dev, rows, width), BF16),
            jax.ShapeDtypeStruct((per_dev, rows, width), BF16),
            jax.ShapeDtypeStruct((per_dev, rows, 3 * hid_pad), BF16),
        ),
        in_specs=[vmem, vmem, hbm, hbm, hbm],
        out_specs=(vmem, hbm, hbm, hbm),
        scratch_shapes=[pltpu.VMEM(shape, dtype) for shape, dtype in scratch]
        + [
            dma((3,)),
            dma((2, 2, owners)),
            dma((2, 2, owners)),
            dma((2, owners)),
            dma((2, owners)),
            dma((per_dev,)),
            dma((per_dev,)),
            dma((3, per_dev)),
            dma((owners,)),
            dma((owners,)),
            dma((owners,)),
            dma((owners,)),
        ],
        compiler_params=pltpu.CompilerParams(
            collective_id=0, has_side_effects=True, vmem_limit_bytes=62 * 2**20
        ),
        name="route",
    )(tok_in, out_grad, gate_weight, up_weight, down_weight)

    def one(a, b):
        return pl.BlockSpec((1, a, b), lambda e: (e, 0, 0))

    grads = pl.pallas_call(
        functools.partial(weights_kernel, hid, hid_pad),
        grid=(per_dev,),
        out_shape=(
            jax.ShapeDtypeStruct(gate_weight.shape, BF16),
            jax.ShapeDtypeStruct(up_weight.shape, BF16),
            jax.ShapeDtypeStruct(down_weight.shape, BF16),
        ),
        in_specs=[one(rows, width), one(rows, width), one(rows, 3 * hid_pad)],
        out_specs=(one(width, hid), one(width, hid), one(hid, width)),
        compiler_params=pltpu.CompilerParams(vmem_limit_bytes=32 * 2**20),
        name="weight_grads",
    )(xs, dr, back)
    return (
        out[:tok_rows].astype(BF16),
        out[tok_rows : tok_rows + top_count, :tok_rows].T,
        *grads,
    )


def solution(mesh):
    placed = (
        P(("groups", "expert", "dp"), "inner"),
        P(("groups", "expert", "dp"), "inner"),
        P(("groups", "expert", "dp"), None),
        P(("groups", "expert", "dp"), None),
        P("expert", "inner", "dp"),
        P("expert", "inner", "dp"),
        P("expert", "dp", "inner"),
    )
    return jax.shard_map(
        on_device,
        mesh=mesh,
        in_specs=placed,
        out_specs=(
            P(("groups", "expert", "dp"), "inner"),
            P(("groups", "expert", "dp"), None),
            P(("groups", "expert"), "inner", "dp"),
            P(("groups", "expert"), "inner", "dp"),
            P(("groups", "expert"), "dp", "inner"),
        ),
        check_vma=False,
    )
```

```python
import functools

import jax
import jax.numpy as jnp
from jax import lax
from jax.experimental import pallas as pl
from jax.experimental.pallas import tpu as pltpu
from jax.sharding import PartitionSpec as P

F32 = jnp.float32
BF16 = jnp.bfloat16


def select_rows(packed, width, top_count, per_dev, block_rows, capacity):
    total = packed.shape[0]
    blocks = total // block_rows
    run = 4 if blocks % 4 == 0 else 1
    runs = blocks // run
    span = run * block_rows
    rows = -(-run * capacity // 16) * 16
    ids = packed[:, 2 * width : 2 * width + top_count].astype(jnp.int32)
    probs = packed[:, 2 * width + top_count : 2 * width + 2 * top_count]
    mine = lax.axis_index("expert") * per_dev + jnp.arange(per_dev, dtype=jnp.int32)
    hits = ids[:, :, None] == mine[None, None, :]
    member = jnp.any(hits, axis=1).reshape(runs, span, per_dev)
    weight = jnp.sum(jnp.where(hits, probs[:, :, None].astype(F32), 0.0), axis=1)
    weight = weight.reshape(runs, span, per_dev)
    at = jnp.arange(span, dtype=jnp.int32)
    earlier = (at[:, None] > at[None, :]).astype(BF16)
    slot = jnp.einsum("ts,gse->get", earlier, member.astype(BF16), preferred_element_type=F32)
    slot = jnp.where(member.transpose(0, 2, 1), slot.astype(jnp.int32), -1)
    places = jnp.arange(rows, dtype=jnp.int32)
    picked = slot[:, :, None, :] == places[None, None, :, None]
    row_prob = jnp.sum(jnp.where(picked, weight.transpose(0, 2, 1)[:, :, None, :], 0.0), axis=3)
    return picked.astype(BF16), row_prob, hits, runs, span, rows


def on_device_wide(tokens, out_grad, expert_ids, gate_probs, gate_weight, up_weight, down_weight):
    tok_rows, width = tokens.shape
    top_count = expert_ids.shape[1]
    per_dev = gate_weight.shape[0]
    experts = per_dev * lax.axis_size("expert")
    capacity = tok_rows * top_count // experts + 1
    packed = jnp.concatenate(
        [tokens, out_grad, expert_ids.astype(BF16), gate_probs.astype(BF16)], axis=1
    )
    packed = lax.all_gather(packed, ("expert", "dp"), axis=0, tiled=True)
    picked, row_prob, hits, runs, span, rows = select_rows(
        packed, width, top_count, per_dev, tok_rows, capacity
    )
    both = packed[:, : 2 * width].reshape(runs, span, 2 * width)
    sorted_rows = jnp.einsum("gest,gtd->egsd", picked, both, preferred_element_type=F32)
    sorted_rows = sorted_rows.astype(BF16).reshape(per_dev, runs * rows, 2 * width)
    expert_rows, expert_grads = sorted_rows[:, :, :width], sorted_rows[:, :, width:]
    prob_col = row_prob.transpose(1, 0, 2).reshape(per_dev, runs * rows, 1)
    hid = gate_weight.shape[2]
    parts = jnp.concatenate(
        [
            jnp.einsum("jrd,jdf->jrf", expert_rows, gate_weight, preferred_element_type=F32),
            jnp.einsum("jrd,jdf->jrf", expert_rows, up_weight, preferred_element_type=F32),
            jnp.einsum("jrd,jfd->jrf", expert_grads, down_weight, preferred_element_type=F32),
        ],
        axis=2,
    ).astype(BF16)
    sums = lax.psum(parts, "inner").astype(F32)
    gate, up, slope = sums[..., :hid], sums[..., hid : 2 * hid], sums[..., 2 * hid :]
    sig = jax.nn.sigmoid(gate)
    act = gate * sig
    hidden = (act * up).astype(BF16)
    scores = jnp.sum(hidden.astype(F32) * slope, axis=-1)
    hidden_grad = prob_col * slope
    gate_back = (hidden_grad * up * sig * (1.0 + gate * (1.0 - sig))).astype(BF16)
    up_back = (hidden_grad * act).astype(BF16)
    row_grads = jnp.einsum("jrf,jdf->jrd", gate_back, gate_weight, preferred_element_type=F32)
    row_grads = (
        row_grads + jnp.einsum("jrf,jdf->jrd", up_back, up_weight, preferred_element_type=F32)
    ).astype(BF16)
    token_part = jnp.einsum(
        "gest,egsd->gtd",
        picked,
        row_grads.reshape(per_dev, runs, rows, width),
        preferred_element_type=F32,
    ).reshape(runs * span, width)
    score_rows = scores.reshape(per_dev, runs, rows).transpose(1, 0, 2)
    score_part = jnp.sum(picked.astype(F32) * score_rows[..., None], axis=2)
    score_part = score_part.transpose(0, 2, 1).reshape(runs * span, 1, per_dev)
    score_part = jnp.sum(jnp.where(hits, score_part, 0.0), axis=2)
    returned = lax.psum_scatter(
        jnp.concatenate([token_part, score_part], axis=1).astype(BF16),
        ("expert", "dp"),
        scatter_dimension=0,
        tiled=True,
    )
    grad_gate = jnp.einsum("jrd,jrf->jdf", expert_rows, gate_back, preferred_element_type=F32)
    grad_up = jnp.einsum("jrd,jrf->jdf", expert_rows, up_back, preferred_element_type=F32)
    down_rows = (prob_col * expert_grads.astype(F32)).astype(BF16)
    grad_down = jnp.einsum("jrf,jrd->jfd", hidden, down_rows, preferred_element_type=F32)
    return (
        returned[:, :width],
        returned[:, width:].astype(F32),
        grad_gate.astype(BF16),
        grad_up.astype(BF16),
        grad_down.astype(BF16),
    )


MESH = pl.DeviceIdType.MESH
PAD = 16
TRANS_LHS = (((0,), (0,)), ((), ()))
TRANS_RHS = (((1,), (1,)), ((), ()))


def dot_t(a, b, dims):
    return lax.dot_general(a, b, dims, preferred_element_type=F32)


def route_kernel(
    owners, run, slots, top_count,
    tok_in, grad_in, gw_hbm, uw_hbm, dw_hbm,
    out, xs_hbm, gs_hbm, back_hbm,
    tok, grd, gw, uw, dw, xs, gs, onehot, prob, part, peer, part_s, peer_s, back, rowg,
    pair, chosen, tp, rx, rz,
    w_sem, send_z, recv_z, send_x, recv_x, send_i, recv_i, send_s, recv_s, o_sem,
    send_a, recv_a, send_b, recv_b,
):
    m = lax.axis_index("expert")
    j = lax.axis_index("dp")
    i = lax.axis_index("inner")
    blocks, tall, width = tok.shape
    rows_blk = tall - PAD
    per_dev, rows, _ = xs.shape
    hid = gw.shape[1]
    hid_pad = part_s.shape[2]
    runs = blocks // run
    span = run * rows_blk
    x_dev, i_dev = {"dp": 1 - j}, {"inner": 1 - i}

    loads = [
        pltpu.make_async_copy(s, d, w_sem.at[n])
        for n, (s, d) in enumerate(((gw_hbm, gw), (uw_hbm, uw), (dw_hbm, dw)))
    ]
    for load in loads:
        load.start()

    barrier = pltpu.get_barrier_semaphore()
    pl.semaphore_signal(barrier, inc=1, device_id=x_dev, device_id_type=MESH)
    pl.semaphore_signal(barrier, inc=1, device_id=i_dev, device_id_type=MESH)
    for d in range(1, owners):
        pl.semaphore_signal(
            barrier, inc=1, device_id={"expert": lax.rem(m + d, owners)}, device_id_type=MESH
        )
    pl.semaphore_wait(barrier, owners + 1)

    bufs = (tok, grd)
    own = (tok_in, grad_in)

    def hop(c, origin, right, step):
        block = 2 * origin + j
        lane = 0 if right else 1
        return pltpu.make_async_remote_copy(
            src_ref=own[c] if step == 0 else bufs[c].at[block],
            dst_ref=bufs[c].at[block],
            send_sem=send_z.at[c, lane, step],
            recv_sem=recv_z.at[c, lane, step],
            device_id={"expert": jnp.clip(m + 1 if right else m - 1, 0, owners - 1)},
            device_id_type=MESH,
        )

    def cross(c, origin, block_j, mine):
        return pltpu.make_async_remote_copy(
            src_ref=own[c] if mine else bufs[c].at[2 * origin + block_j],
            dst_ref=bufs[c].at[2 * origin + block_j],
            send_sem=send_x.at[c, origin],
            recv_sem=recv_x.at[c, origin],
            device_id=x_dev,
            device_id_type=MESH,
        )

    def can_send(right, origin):
        if right:
            return (m + 1 < owners) & (origin >= 0)
        return (m >= 1) & (origin < owners)

    def begin(c):
        for right in (True, False):
            @pl.when(can_send(right, m))
            def _(right=right):
                hop(c, m, right, 0).start()
        cross(c, m, j, True).start()

    def advance(c, step):
        for right in (True, False):
            origin = m - step if right else m + step

            @pl.when((origin >= 0) & (origin < owners))
            def _(right=right, origin=origin):
                hop(c, origin, right, step - 1).wait_recv()
                if step < owners - 1:
                    @pl.when(can_send(right, origin))
                    def _():
                        hop(c, origin, right, step).start()
                cross(c, origin, j, False).start()

    begin(0)
    tok[2 * m + j] = tok_in[...]
    for step in range(1, owners):
        advance(0, step)
        if step == max(1, owners - 2):
            begin(1)
    grd[2 * m + j] = grad_in[...]
    pending = list(range(1, owners))

    def advance_next():
        if pending:
            advance(1, pending.pop(0))

    at = lax.broadcasted_iota(jnp.int32, (span, span), 0)
    to = lax.broadcasted_iota(jnp.int32, (span, span), 1)
    earlier = (at < to).astype(BF16)
    place = lax.broadcasted_iota(jnp.int32, (slots, span), 0)
    expert_of = lax.broadcasted_iota(jnp.int32, (per_dev, span), 0) + m * per_dev

    def ids_of(g):
        return jnp.concatenate(
            [tok[g * run + b, rows_blk:tall, :rows_blk].astype(F32) for b in range(run)], axis=1
        )

    for o in range(owners):
        cross(0, o, 1 - j, False).wait_recv()
    for g in range(runs):
        meta = ids_of(g)
        ids = meta.astype(jnp.int32)
        member = jnp.zeros((per_dev, span), F32)
        weight = jnp.zeros((per_dev, span), F32)
        for k in range(top_count):
            hit = expert_of == ids[k : k + 1, :]
            member = member + jnp.where(hit, 1.0, 0.0)
            weight = weight + jnp.where(hit, meta[top_count + k : top_count + k + 1, :], 0.0)
        slot = jnp.dot(member.astype(BF16), earlier, preferred_element_type=F32).astype(jnp.int32)
        slot = jnp.where(member > 0.5, slot, -1)
        chosen[g] = ids[:top_count, :]
        for e in range(per_dev):
            hit = place == slot[e : e + 1, :]
            onehot[g, e] = jnp.where(hit, 1.0, 0.0).astype(BF16)
            prob[e, g * slots : (g + 1) * slots, :] = jnp.sum(
                jnp.where(hit, weight[e : e + 1, :], 0.0), axis=1, keepdims=True
            )
        advance_next()

    batch = 4 if per_dev % 4 == 0 else 1

    def spread(buf, dest):
        for g in range(runs):
            whole = buf[g * run : (g + 1) * run, :rows_blk, :].reshape(span, width)

            @pl.loop(0, per_dev // batch)
            def _(n):
                pick = onehot[g, pl.ds(n * batch, batch)].reshape(batch * slots, span)
                got = jnp.dot(pick, whole, preferred_element_type=F32).astype(BF16)
                dest[pl.ds(n * batch, batch), g * slots : (g + 1) * slots, :] = got.reshape(
                    batch, slots, width
                )

    spread(tok, xs)
    xs_out = pltpu.make_async_copy(xs, xs_hbm, o_sem.at[1, 0])
    xs_out.start()
    while pending:
        advance_next()
    for load in loads:
        load.wait()

    def swap(e):
        return pltpu.make_async_remote_copy(
            src_ref=part.at[e], dst_ref=peer.at[e],
            send_sem=send_i.at[e], recv_sem=recv_i.at[e],
            device_id=i_dev, device_id_type=MESH,
        )

    def swap_s(e):
        return pltpu.make_async_remote_copy(
            src_ref=part_s.at[e], dst_ref=peer_s.at[e],
            send_sem=send_s.at[e], recv_sem=recv_s.at[e],
            device_id=i_dev, device_id_type=MESH,
        )

    @pl.loop(0, per_dev)
    def _(e):
        rows_e = xs[e]
        part[e, :, 0:hid] = dot_t(rows_e, gw[e], TRANS_RHS).astype(BF16)
        part[e, :, hid_pad : hid_pad + hid] = dot_t(rows_e, uw[e], TRANS_RHS).astype(BF16)
        swap(e).start()

    for o in range(owners):
        cross(1, o, 1 - j, False).wait_recv()
    spread(grd, gs)
    gs_out = pltpu.make_async_copy(gs, gs_hbm, o_sem.at[1, 1])
    gs_out.start()

    @pl.loop(0, per_dev)
    def _(e):
        part_s[e, :, 0:hid] = dot_t(gs[e], dw[e], TRANS_RHS).astype(BF16)
        swap_s(e).start()

    pair[...] = jnp.zeros_like(pair)

    def back_out(e):
        return pltpu.make_async_copy(back.at[e], back_hbm.at[e], o_sem.at[0, e])

    @pl.loop(0, per_dev)
    def _(e):
        swap(e).wait()
        swap_s(e).wait()

        def total(mine, theirs, n):
            cols = slice(n * hid_pad, n * hid_pad + hid)
            return mine[e, :, cols].astype(F32) + theirs[e, :, cols].astype(F32)

        gate, up = total(part, peer, 0), total(part, peer, 1)
        slope = total(part_s, peer_s, 0)
        col = prob[e]
        sig = jax.nn.sigmoid(gate)
        act = gate * sig
        hidden = (act * up).astype(BF16).astype(F32)
        score = jnp.sum(hidden * slope, axis=1, keepdims=True)
        hidden_grad = col * slope
        gate_back = (hidden_grad * up * sig * (1.0 + gate * (1.0 - sig))).astype(BF16)
        up_back = (hidden_grad * act).astype(BF16)
        back[e, :, 0:hid] = gate_back
        back[e, :, hid_pad : hid_pad + hid] = up_back
        back[e, :, 2 * hid_pad : 2 * hid_pad + hid] = (col * hidden).astype(BF16)
        back_out(e).start()
        rowg[e] = (
            jnp.dot(gate_back, gw[e], preferred_element_type=F32)
            + jnp.dot(up_back, uw[e], preferred_element_type=F32)
        ).astype(BF16)
        for g in range(runs):
            seen = jnp.sum(
                onehot[g, e].astype(F32) * score[g * slots : (g + 1) * slots, :],
                axis=0, keepdims=True,
            )
            pair[g] += jnp.where(chosen[g] == m * per_dev + e, seen, 0.0)

    def give(o):
        return pltpu.make_async_remote_copy(
            src_ref=tp.at[2 * o + 1 - j], dst_ref=rx.at[o],
            send_sem=send_a.at[o], recv_sem=recv_a.at[o],
            device_id=x_dev, device_id_type=MESH,
        )

    def deliver(o, slot_at):
        return pltpu.make_async_remote_copy(
            src_ref=tp.at[2 * o + j], dst_ref=rz.at[slot_at],
            send_sem=send_b.at[o], recv_sem=recv_b.at[slot_at],
            device_id={"expert": o}, device_id_type=MESH,
        )

    order = []
    for k in range(owners):
        found, at_k = m * 0, m * 0
        for d in range(owners - 1, -1, -1):
            for cand in (m + d, m - d) if d else (m,):
                valid = (cand >= 0) & (cand < owners)
                at_k = jnp.where(valid & (found == k), cand, at_k)
                found = found + jnp.where(valid, 1, 0)
        order.append(at_k)

    def combine(n):
        g, b = n // run, n % run
        rows_at = pl.ds(pl.multiple_of(g * slots, 16), slots)
        cols = pl.ds(pl.multiple_of(b * rows_blk, 128), rows_blk)
        mine = rowg[:, rows_at, :].reshape(per_dev * slots, width)
        pick = onehot[g, :, :, cols].reshape(per_dev * slots, rows_blk)
        tp[n, 0:rows_blk, :] = dot_t(pick, mine, TRANS_LHS).astype(BF16)
        tp[n, rows_blk:tall, :] = jnp.zeros((PAD, width), BF16)
        tp[n, rows_blk:tall, 0:rows_blk] = jnp.concatenate(
            [pair[g, :, cols], jnp.zeros((PAD - top_count, rows_blk), F32)], axis=0
        ).astype(BF16)

    for o in order:
        combine(2 * o + 1 - j)
        give(o).start()
    for k, o in enumerate(order):
        combine(2 * o + j)
        give(o).wait_recv()
        if k < owners - 1:
            tp[2 * o + j] = (tp[2 * o + j].astype(F32) + rx[o].astype(F32)).astype(BF16)
            deliver(o, m).start()
        else:
            out[...] = tp[2 * o + j].astype(F32) + rx[o].astype(F32)
    for o in order[:-1]:
        deliver(o, o).wait_recv()
        out[...] += rz[o].astype(F32)

    for o in range(owners):
        give(o).wait_send()

        @pl.when(o != m)
        def _(o=o):
            deliver(o, o).wait_send()
        for c in range(2):
            cross(c, o, j, False).wait_send()
    for step in range(owners - 1):
        for c in range(2):
            for right in (True, False):
                origin = m - step if right else m + step

                @pl.when(can_send(right, origin))
                def _(c=c, right=right, origin=origin, step=step):
                    hop(c, origin, right, step).wait_send()
    xs_out.wait()
    gs_out.wait()

    @pl.loop(0, per_dev)
    def _(e):
        back_out(e).wait()


def weights_kernel(hid, hid_pad, xs, gs, back, gate_out, up_out, down_out):
    rows_e = xs[0]
    gate_out[0] = dot_t(back[0, :, 0:hid], rows_e, TRANS_LHS).astype(BF16)
    up_out[0] = dot_t(back[0, :, hid_pad : hid_pad + hid], rows_e, TRANS_LHS).astype(BF16)
    down_out[0] = dot_t(back[0, :, 2 * hid_pad : 2 * hid_pad + hid], gs[0], TRANS_LHS).astype(BF16)


def on_device(tokens, out_grad, expert_ids, gate_probs, gate_weight, up_weight, down_weight):
    args = (tokens, out_grad, expert_ids, gate_probs, gate_weight, up_weight, down_weight)
    tok_rows, width = tokens.shape
    top_count = expert_ids.shape[1]
    per_dev, _, hid = gate_weight.shape
    owners = lax.axis_size("expert")
    blocks = owners * lax.axis_size("dp")
    capacity = tok_rows * top_count // (per_dev * owners) + 1
    run = 4 if blocks % 4 == 0 else 2
    runs = blocks // run
    slots = -(-run * capacity // 16) * 16
    rows = runs * slots
    hid_pad = -(-hid // 128) * 128
    tall = tok_rows + PAD
    scratch = [
        ((blocks, tall, width), BF16),
        ((blocks, tok_rows, width), BF16),
        (down_weight.shape, BF16),
        (down_weight.shape, BF16),
        (down_weight.shape, BF16),
        ((per_dev, rows, width), BF16),
        ((per_dev, rows, width), BF16),
        ((runs, per_dev, slots, run * tok_rows), BF16),
        ((per_dev, rows, 1), F32),
        ((per_dev, rows, 2 * hid_pad), BF16),
        ((per_dev, rows, 2 * hid_pad), BF16),
        ((per_dev, rows, hid_pad), BF16),
        ((per_dev, rows, hid_pad), BF16),
        ((per_dev, rows, 3 * hid_pad), BF16),
        ((per_dev, rows, width), BF16),
        ((runs, top_count, run * tok_rows), F32),
        ((runs, top_count, run * tok_rows), jnp.int32),
        ((blocks, tall, width), BF16),
        ((owners, tall, width), BF16),
        ((owners, tall, width), BF16),
    ]
    need = 0
    for shape, dtype in scratch:
        lanes = -(-shape[-1] // 128) * 128
        size = lanes * (2 if dtype == BF16 else 4)
        for n in shape[:-1]:
            size *= n
        need += size
    fits = need < 57 * 2**20 and lax.axis_size("dp") == 2 and lax.axis_size("inner") == 2
    fits = fits and owners > 1 and tok_rows == 128 and top_count == 8
    if not fits:
        return on_device_wide(*args)
    meta = jnp.concatenate([expert_ids.astype(BF16).T, gate_probs.astype(BF16).T], axis=0)
    tok_in = jnp.concatenate([tokens, jnp.pad(meta, ((0, 0), (0, width - tok_rows)))], axis=0)
    vmem = pl.BlockSpec(memory_space=pltpu.VMEM)
    hbm = pl.BlockSpec(memory_space=pl.ANY)
    dma = pltpu.SemaphoreType.DMA
    out, xs, gs, back = pl.pallas_call(
        functools.partial(route_kernel, owners, run, slots, top_count),
        out_shape=(
            jax.ShapeDtypeStruct((tall, width), F32),
            jax.ShapeDtypeStruct((per_dev, rows, width), BF16),
            jax.ShapeDtypeStruct((per_dev, rows, width), BF16),
            jax.ShapeDtypeStruct((per_dev, rows, 3 * hid_pad), BF16),
        ),
        in_specs=[vmem, vmem, hbm, hbm, hbm],
        out_specs=(vmem, hbm, hbm, hbm),
        scratch_shapes=[pltpu.VMEM(shape, dtype) for shape, dtype in scratch]
        + [
            dma((3,)),
            dma((2, 2, owners)),
            dma((2, 2, owners)),
            dma((2, owners)),
            dma((2, owners)),
            dma((per_dev,)),
            dma((per_dev,)),
            dma((per_dev,)),
            dma((per_dev,)),
            dma((2, max(per_dev, 2))),
            dma((owners,)),
            dma((owners,)),
            dma((owners,)),
            dma((owners,)),
        ],
        compiler_params=pltpu.CompilerParams(
            collective_id=0, has_side_effects=True, vmem_limit_bytes=62 * 2**20
        ),
        name="route",
    )(tok_in, out_grad, gate_weight.transpose(0, 2, 1), up_weight.transpose(0, 2, 1), down_weight)

    def one(a, b):
        return pl.BlockSpec((1, a, b), lambda e: (e, 0, 0))

    grad_gate, grad_up, grad_down = pl.pallas_call(
        functools.partial(weights_kernel, hid, hid_pad),
        grid=(per_dev,),
        out_shape=(jax.ShapeDtypeStruct(down_weight.shape, BF16),) * 3,
        in_specs=[one(rows, width), one(rows, width), one(rows, 3 * hid_pad)],
        out_specs=(one(hid, width),) * 3,
        compiler_params=pltpu.CompilerParams(vmem_limit_bytes=60 * 2**20),
        name="weight_grads",
    )(xs, gs, back)
    return (
        out[:tok_rows].astype(BF16),
        out[tok_rows : tok_rows + top_count, :tok_rows].T,
        grad_gate.transpose(0, 2, 1),
        grad_up.transpose(0, 2, 1),
        grad_down,
    )


def solution(mesh):
    placed = (
        P(("groups", "expert", "dp"), "inner"),
        P(("groups", "expert", "dp"), "inner"),
        P(("groups", "expert", "dp"), None),
        P(("groups", "expert", "dp"), None),
        P("expert", "inner", "dp"),
        P("expert", "inner", "dp"),
        P("expert", "dp", "inner"),
    )
    return jax.shard_map(
        on_device,
        mesh=mesh,
        in_specs=placed,
        out_specs=(
            P(("groups", "expert", "dp"), "inner"),
            P(("groups", "expert", "dp"), None),
            P(("groups", "expert"), "inner", "dp"),
            P(("groups", "expert"), "inner", "dp"),
            P(("groups", "expert"), "dp", "inner"),
        ),
        check_vma=False,
    )
```

```python
import functools

import jax
import jax.numpy as jnp
from jax import lax
from jax.experimental import pallas as pl
from jax.experimental.pallas import tpu as pltpu
from jax.sharding import PartitionSpec as P

F32 = jnp.float32
BF16 = jnp.bfloat16


def select_rows(packed, width, top_count, per_dev, block_rows, capacity):
    total = packed.shape[0]
    blocks = total // block_rows
    run = 4 if blocks % 4 == 0 else 1
    runs = blocks // run
    span = run * block_rows
    rows = -(-run * capacity // 16) * 16
    ids = packed[:, 2 * width : 2 * width + top_count].astype(jnp.int32)
    probs = packed[:, 2 * width + top_count : 2 * width + 2 * top_count]
    mine = lax.axis_index("expert") * per_dev + jnp.arange(per_dev, dtype=jnp.int32)
    hits = ids[:, :, None] == mine[None, None, :]
    member = jnp.any(hits, axis=1).reshape(runs, span, per_dev)
    weight = jnp.sum(jnp.where(hits, probs[:, :, None].astype(F32), 0.0), axis=1)
    weight = weight.reshape(runs, span, per_dev)
    at = jnp.arange(span, dtype=jnp.int32)
    earlier = (at[:, None] > at[None, :]).astype(BF16)
    slot = jnp.einsum("ts,gse->get", earlier, member.astype(BF16), preferred_element_type=F32)
    slot = jnp.where(member.transpose(0, 2, 1), slot.astype(jnp.int32), -1)
    places = jnp.arange(rows, dtype=jnp.int32)
    picked = slot[:, :, None, :] == places[None, None, :, None]
    row_prob = jnp.sum(jnp.where(picked, weight.transpose(0, 2, 1)[:, :, None, :], 0.0), axis=3)
    return picked.astype(BF16), row_prob, hits, runs, span, rows


def on_device_wide(tokens, out_grad, expert_ids, gate_probs, gate_weight, up_weight, down_weight):
    tok_rows, width = tokens.shape
    top_count = expert_ids.shape[1]
    per_dev = gate_weight.shape[0]
    experts = per_dev * lax.axis_size("expert")
    capacity = tok_rows * top_count // experts + 1
    packed = jnp.concatenate(
        [tokens, out_grad, expert_ids.astype(BF16), gate_probs.astype(BF16)], axis=1
    )
    packed = lax.all_gather(packed, ("expert", "dp"), axis=0, tiled=True)
    picked, row_prob, hits, runs, span, rows = select_rows(
        packed, width, top_count, per_dev, tok_rows, capacity
    )
    both = packed[:, : 2 * width].reshape(runs, span, 2 * width)
    sorted_rows = jnp.einsum("gest,gtd->egsd", picked, both, preferred_element_type=F32)
    sorted_rows = sorted_rows.astype(BF16).reshape(per_dev, runs * rows, 2 * width)
    expert_rows, expert_grads = sorted_rows[:, :, :width], sorted_rows[:, :, width:]
    prob_col = row_prob.transpose(1, 0, 2).reshape(per_dev, runs * rows, 1)
    hid = gate_weight.shape[2]
    parts = jnp.concatenate(
        [
            jnp.einsum("jrd,jdf->jrf", expert_rows, gate_weight, preferred_element_type=F32),
            jnp.einsum("jrd,jdf->jrf", expert_rows, up_weight, preferred_element_type=F32),
            jnp.einsum("jrd,jfd->jrf", expert_grads, down_weight, preferred_element_type=F32),
        ],
        axis=2,
    ).astype(BF16)
    sums = lax.psum(parts, "inner").astype(F32)
    gate, up, slope = sums[..., :hid], sums[..., hid : 2 * hid], sums[..., 2 * hid :]
    sig = jax.nn.sigmoid(gate)
    act = gate * sig
    hidden = (act * up).astype(BF16)
    scores = jnp.sum(hidden.astype(F32) * slope, axis=-1)
    hidden_grad = prob_col * slope
    gate_back = (hidden_grad * up * sig * (1.0 + gate * (1.0 - sig))).astype(BF16)
    up_back = (hidden_grad * act).astype(BF16)
    row_grads = jnp.einsum("jrf,jdf->jrd", gate_back, gate_weight, preferred_element_type=F32)
    row_grads = (
        row_grads + jnp.einsum("jrf,jdf->jrd", up_back, up_weight, preferred_element_type=F32)
    ).astype(BF16)
    token_part = jnp.einsum(
        "gest,egsd->gtd",
        picked,
        row_grads.reshape(per_dev, runs, rows, width),
        preferred_element_type=F32,
    ).reshape(runs * span, width)
    score_rows = scores.reshape(per_dev, runs, rows).transpose(1, 0, 2)
    score_part = jnp.sum(picked.astype(F32) * score_rows[..., None], axis=2)
    score_part = score_part.transpose(0, 2, 1).reshape(runs * span, 1, per_dev)
    score_part = jnp.sum(jnp.where(hits, score_part, 0.0), axis=2)
    returned = lax.psum_scatter(
        jnp.concatenate([token_part, score_part], axis=1).astype(BF16),
        ("expert", "dp"),
        scatter_dimension=0,
        tiled=True,
    )
    grad_gate = jnp.einsum("jrd,jrf->jdf", expert_rows, gate_back, preferred_element_type=F32)
    grad_up = jnp.einsum("jrd,jrf->jdf", expert_rows, up_back, preferred_element_type=F32)
    down_rows = (prob_col * expert_grads.astype(F32)).astype(BF16)
    grad_down = jnp.einsum("jrf,jrd->jfd", hidden, down_rows, preferred_element_type=F32)
    return (
        returned[:, :width],
        returned[:, width:].astype(F32),
        grad_gate.astype(BF16),
        grad_up.astype(BF16),
        grad_down.astype(BF16),
    )


MESH = pl.DeviceIdType.MESH
PAD = 16
TRANS_LHS = (((0,), (0,)), ((), ()))
TRANS_RHS = (((1,), (1,)), ((), ()))


def dot_t(a, b, dims):
    return lax.dot_general(a, b, dims, preferred_element_type=F32)


def route_kernel(
    owners, run, slots, top_count,
    tok_in, grad_in, gw_hbm, uw_hbm, dw_hbm,
    out, xs_hbm, gs_hbm, back_hbm,
    tok, grd, gw, uw, dw, xs, gs, onehot, prob, part, peer, part_s, peer_s, back, rowg,
    pair, chosen, tp, rx, rz,
    w_sem, send_z, recv_z, send_x, recv_x, send_i, recv_i, send_s, recv_s, o_sem,
    send_a, recv_a, send_b, recv_b,
):
    m = lax.axis_index("expert")
    j = lax.axis_index("dp")
    i = lax.axis_index("inner")
    blocks, tall, width = tok.shape
    rows_blk = tall - PAD
    per_dev, rows, _ = xs.shape
    hid = gw.shape[1]
    hid_pad = part_s.shape[2]
    runs = blocks // run
    span = run * rows_blk
    x_dev, i_dev = {"dp": 1 - j}, {"inner": 1 - i}

    loads = [
        pltpu.make_async_copy(s, d, w_sem.at[n])
        for n, (s, d) in enumerate(((gw_hbm, gw), (uw_hbm, uw), (dw_hbm, dw)))
    ]
    for load in loads:
        load.start()

    barrier = pltpu.get_barrier_semaphore()
    pl.semaphore_signal(barrier, inc=1, device_id=x_dev, device_id_type=MESH)
    pl.semaphore_signal(barrier, inc=1, device_id=i_dev, device_id_type=MESH)
    for d in range(1, owners):
        pl.semaphore_signal(
            barrier, inc=1, device_id={"expert": lax.rem(m + d, owners)}, device_id_type=MESH
        )
    pl.semaphore_wait(barrier, owners + 1)

    bufs = (tok, grd)
    own = (tok_in, grad_in)

    def hop(c, origin, right, step):
        block = 2 * origin + j
        lane = 0 if right else 1
        return pltpu.make_async_remote_copy(
            src_ref=own[c] if step == 0 else bufs[c].at[block],
            dst_ref=bufs[c].at[block],
            send_sem=send_z.at[c, lane, step],
            recv_sem=recv_z.at[c, lane, step],
            device_id={"expert": jnp.clip(m + 1 if right else m - 1, 0, owners - 1)},
            device_id_type=MESH,
        )

    def cross(c, origin, block_j, mine):
        return pltpu.make_async_remote_copy(
            src_ref=own[c] if mine else bufs[c].at[2 * origin + block_j],
            dst_ref=bufs[c].at[2 * origin + block_j],
            send_sem=send_x.at[c, origin],
            recv_sem=recv_x.at[c, origin],
            device_id=x_dev,
            device_id_type=MESH,
        )

    def can_send(right, origin):
        if right:
            return (m + 1 < owners) & (origin >= 0)
        return (m >= 1) & (origin < owners)

    def begin(c):
        for right in (True, False):
            @pl.when(can_send(right, m))
            def _(right=right):
                hop(c, m, right, 0).start()
        cross(c, m, j, True).start()

    def advance(c, step):
        for right in (True, False):
            origin = m - step if right else m + step

            @pl.when((origin >= 0) & (origin < owners))
            def _(right=right, origin=origin):
                hop(c, origin, right, step - 1).wait_recv()
                if step < owners - 1:
                    @pl.when(can_send(right, origin))
                    def _():
                        hop(c, origin, right, step).start()
                cross(c, origin, j, False).start()

    begin(0)
    tok[2 * m + j] = tok_in[...]
    for step in range(1, owners):
        advance(0, step)
        if step == max(1, owners - 2):
            begin(1)
    grd[2 * m + j] = grad_in[...]
    pending = list(range(1, owners))

    def advance_next():
        if pending:
            advance(1, pending.pop(0))

    at = lax.broadcasted_iota(jnp.int32, (span, span), 0)
    to = lax.broadcasted_iota(jnp.int32, (span, span), 1)
    earlier = (at < to).astype(BF16)
    place = lax.broadcasted_iota(jnp.int32, (slots, span), 0)
    expert_of = lax.broadcasted_iota(jnp.int32, (per_dev, span), 0) + m * per_dev

    def ids_of(g):
        return jnp.concatenate(
            [tok[g * run + b, rows_blk:tall, :rows_blk].astype(F32) for b in range(run)], axis=1
        )

    for o in range(owners):
        cross(0, o, 1 - j, False).wait_recv()
    for g in range(runs):
        meta = ids_of(g)
        ids = meta.astype(jnp.int32)
        member = jnp.zeros((per_dev, span), F32)
        weight = jnp.zeros((per_dev, span), F32)
        for k in range(top_count):
            hit = expert_of == ids[k : k + 1, :]
            member = member + jnp.where(hit, 1.0, 0.0)
            weight = weight + jnp.where(hit, meta[top_count + k : top_count + k + 1, :], 0.0)
        slot = jnp.dot(member.astype(BF16), earlier, preferred_element_type=F32).astype(jnp.int32)
        slot = jnp.where(member > 0.5, slot, -1)
        chosen[g] = ids[:top_count, :]
        for e in range(per_dev):
            hit = place == slot[e : e + 1, :]
            onehot[g, e] = jnp.where(hit, 1.0, 0.0).astype(BF16)
            prob[e, g * slots : (g + 1) * slots, :] = jnp.sum(
                jnp.where(hit, weight[e : e + 1, :], 0.0), axis=1, keepdims=True
            )
        advance_next()

    batch = 4 if per_dev % 4 == 0 else 1

    def spread(buf, dest):
        for g in range(runs):
            whole = buf[g * run : (g + 1) * run, :rows_blk, :].reshape(span, width)

            @pl.loop(0, per_dev // batch)
            def _(n):
                pick = onehot[g, pl.ds(n * batch, batch)].reshape(batch * slots, span)
                got = jnp.dot(pick, whole, preferred_element_type=F32).astype(BF16)
                dest[pl.ds(n * batch, batch), g * slots : (g + 1) * slots, :] = got.reshape(
                    batch, slots, width
                )

    spread(tok, xs)
    xs_out = pltpu.make_async_copy(xs, xs_hbm, o_sem.at[1, 0])
    xs_out.start()
    while pending:
        advance_next()
    for load in loads:
        load.wait()

    def swap(e):
        return pltpu.make_async_remote_copy(
            src_ref=part.at[e], dst_ref=peer.at[e],
            send_sem=send_i.at[e], recv_sem=recv_i.at[e],
            device_id=i_dev, device_id_type=MESH,
        )

    def swap_s(e):
        return pltpu.make_async_remote_copy(
            src_ref=part_s.at[e], dst_ref=peer_s.at[e],
            send_sem=send_s.at[e], recv_sem=recv_s.at[e],
            device_id=i_dev, device_id_type=MESH,
        )

    @pl.loop(0, per_dev)
    def _(e):
        rows_e = xs[e]
        part[e, :, 0:hid] = dot_t(rows_e, gw[e], TRANS_RHS).astype(BF16)
        part[e, :, hid_pad : hid_pad + hid] = dot_t(rows_e, uw[e], TRANS_RHS).astype(BF16)
        swap(e).start()

    for o in range(owners):
        cross(1, o, 1 - j, False).wait_recv()
    spread(grd, gs)
    gs_out = pltpu.make_async_copy(gs, gs_hbm, o_sem.at[1, 1])
    gs_out.start()

    @pl.loop(0, per_dev)
    def _(e):
        part_s[e, :, 0:hid] = dot_t(gs[e], dw[e], TRANS_RHS).astype(BF16)
        swap_s(e).start()

    pair[...] = jnp.zeros_like(pair)

    def back_out(e):
        return pltpu.make_async_copy(back.at[e], back_hbm.at[e], o_sem.at[0, e])

    @pl.loop(0, per_dev)
    def _(e):
        swap(e).wait()
        swap_s(e).wait()

        def total(mine, theirs, n):
            cols = slice(n * hid_pad, n * hid_pad + hid)
            return mine[e, :, cols].astype(F32) + theirs[e, :, cols].astype(F32)

        gate, up = total(part, peer, 0), total(part, peer, 1)
        slope = total(part_s, peer_s, 0)
        col = prob[e]
        sig = jax.nn.sigmoid(gate)
        act = gate * sig
        hidden = (act * up).astype(BF16).astype(F32)
        score = jnp.sum(hidden * slope, axis=1, keepdims=True)
        hidden_grad = col * slope
        gate_back = (hidden_grad * up * sig * (1.0 + gate * (1.0 - sig))).astype(BF16)
        up_back = (hidden_grad * act).astype(BF16)
        back[e, :, 0:hid] = gate_back
        back[e, :, hid_pad : hid_pad + hid] = up_back
        back[e, :, 2 * hid_pad : 2 * hid_pad + hid] = (col * hidden).astype(BF16)
        back_out(e).start()
        rowg[e] = (
            jnp.dot(gate_back, gw[e], preferred_element_type=F32)
            + jnp.dot(up_back, uw[e], preferred_element_type=F32)
        ).astype(BF16)
        for g in range(runs):
            seen = jnp.sum(
                onehot[g, e].astype(F32) * score[g * slots : (g + 1) * slots, :],
                axis=0, keepdims=True,
            )
            pair[g] += jnp.where(chosen[g] == m * per_dev + e, seen, 0.0)

    def give(o):
        return pltpu.make_async_remote_copy(
            src_ref=tp.at[2 * o + 1 - j], dst_ref=rx.at[o],
            send_sem=send_a.at[o], recv_sem=recv_a.at[o],
            device_id=x_dev, device_id_type=MESH,
        )

    def deliver(o, slot_at):
        return pltpu.make_async_remote_copy(
            src_ref=tp.at[2 * o + j], dst_ref=rz.at[slot_at],
            send_sem=send_b.at[o], recv_sem=recv_b.at[slot_at],
            device_id={"expert": o}, device_id_type=MESH,
        )

    order = []
    for k in range(owners):
        found, at_k = m * 0, m * 0
        for d in range(owners - 1, -1, -1):
            for cand in (m + d, m - d) if d else (m,):
                valid = (cand >= 0) & (cand < owners)
                at_k = jnp.where(valid & (found == k), cand, at_k)
                found = found + jnp.where(valid, 1, 0)
        order.append(at_k)

    def combine(n):
        g, b = n // run, n % run
        rows_at = pl.ds(pl.multiple_of(g * slots, 16), slots)
        cols = pl.ds(pl.multiple_of(b * rows_blk, 128), rows_blk)
        mine = rowg[:, rows_at, :].reshape(per_dev * slots, width)
        pick = onehot[g, :, :, cols].reshape(per_dev * slots, rows_blk)
        tp[n, 0:rows_blk, :] = dot_t(pick, mine, TRANS_LHS).astype(BF16)
        tp[n, rows_blk:tall, :] = jnp.zeros((PAD, width), BF16)
        tp[n, rows_blk:tall, 0:rows_blk] = jnp.concatenate(
            [pair[g, :, cols], jnp.zeros((PAD - top_count, rows_blk), F32)], axis=0
        ).astype(BF16)

    for o in order:
        combine(2 * o + 1 - j)
        give(o).start()
    for k, o in enumerate(order):
        combine(2 * o + j)
        give(o).wait_recv()
        if k < owners - 1:
            tp[2 * o + j] = (tp[2 * o + j].astype(F32) + rx[o].astype(F32)).astype(BF16)
            deliver(o, m).start()
        else:
            out[...] = tp[2 * o + j].astype(F32) + rx[o].astype(F32)
    for o in order[:-1]:
        deliver(o, o).wait_recv()
        out[...] += rz[o].astype(F32)

    for o in range(owners):
        give(o).wait_send()

        @pl.when(o != m)
        def _(o=o):
            deliver(o, o).wait_send()
        for c in range(2):
            cross(c, o, j, False).wait_send()
    for step in range(owners - 1):
        for c in range(2):
            for right in (True, False):
                origin = m - step if right else m + step

                @pl.when(can_send(right, origin))
                def _(c=c, right=right, origin=origin, step=step):
                    hop(c, origin, right, step).wait_send()
    xs_out.wait()
    gs_out.wait()

    @pl.loop(0, per_dev)
    def _(e):
        back_out(e).wait()


def weights_kernel(hid, hid_pad, xs, gs, back, gate_out, up_out, down_out):
    for n in range(xs.shape[0]):
        rows_e = xs[n]
        gate_out[n] = dot_t(back[n, :, 0:hid], rows_e, TRANS_LHS).astype(BF16)
        up_out[n] = dot_t(back[n, :, hid_pad : hid_pad + hid], rows_e, TRANS_LHS).astype(BF16)
        down_out[n] = dot_t(
            back[n, :, 2 * hid_pad : 2 * hid_pad + hid], gs[n], TRANS_LHS
        ).astype(BF16)


def on_device(tokens, out_grad, expert_ids, gate_probs, gate_weight, up_weight, down_weight):
    args = (tokens, out_grad, expert_ids, gate_probs, gate_weight, up_weight, down_weight)
    tok_rows, width = tokens.shape
    top_count = expert_ids.shape[1]
    per_dev, _, hid = gate_weight.shape
    owners = lax.axis_size("expert")
    blocks = owners * lax.axis_size("dp")
    capacity = tok_rows * top_count // (per_dev * owners) + 1
    run = 4 if blocks % 4 == 0 else 2
    runs = blocks // run
    slots = -(-run * capacity // 16) * 16
    rows = runs * slots
    hid_pad = -(-hid // 128) * 128
    tall = tok_rows + PAD
    scratch = [
        ((blocks, tall, width), BF16),
        ((blocks, tok_rows, width), BF16),
        (down_weight.shape, BF16),
        (down_weight.shape, BF16),
        (down_weight.shape, BF16),
        ((per_dev, rows, width), BF16),
        ((per_dev, rows, width), BF16),
        ((runs, per_dev, slots, run * tok_rows), BF16),
        ((per_dev, rows, 1), F32),
        ((per_dev, rows, 2 * hid_pad), BF16),
        ((per_dev, rows, 2 * hid_pad), BF16),
        ((per_dev, rows, hid_pad), BF16),
        ((per_dev, rows, hid_pad), BF16),
        ((per_dev, rows, 3 * hid_pad), BF16),
        ((per_dev, rows, width), BF16),
        ((runs, top_count, run * tok_rows), F32),
        ((runs, top_count, run * tok_rows), jnp.int32),
        ((blocks, tall, width), BF16),
        ((owners, tall, width), BF16),
        ((owners, tall, width), BF16),
    ]
    need = 0
    for shape, dtype in scratch:
        lanes = -(-shape[-1] // 128) * 128
        size = lanes * (2 if dtype == BF16 else 4)
        for n in shape[:-1]:
            size *= n
        need += size
    fits = need < 57 * 2**20 and lax.axis_size("dp") == 2 and lax.axis_size("inner") == 2
    fits = fits and owners > 1 and tok_rows == 128 and top_count == 8
    if not fits:
        return on_device_wide(*args)
    meta = jnp.concatenate([expert_ids.astype(BF16).T, gate_probs.astype(BF16).T], axis=0)
    tok_in = jnp.concatenate([tokens, jnp.pad(meta, ((0, 0), (0, width - tok_rows)))], axis=0)
    vmem = pl.BlockSpec(memory_space=pltpu.VMEM)
    hbm = pl.BlockSpec(memory_space=pl.ANY)
    dma = pltpu.SemaphoreType.DMA
    out, xs, gs, back = pl.pallas_call(
        functools.partial(route_kernel, owners, run, slots, top_count),
        out_shape=(
            jax.ShapeDtypeStruct((tall, width), F32),
            jax.ShapeDtypeStruct((per_dev, rows, width), BF16),
            jax.ShapeDtypeStruct((per_dev, rows, width), BF16),
            jax.ShapeDtypeStruct((per_dev, rows, 3 * hid_pad), BF16),
        ),
        in_specs=[vmem, vmem, hbm, hbm, hbm],
        out_specs=(vmem, hbm, hbm, hbm),
        scratch_shapes=[pltpu.VMEM(shape, dtype) for shape, dtype in scratch]
        + [
            dma((3,)),
            dma((2, 2, owners)),
            dma((2, 2, owners)),
            dma((2, owners)),
            dma((2, owners)),
            dma((per_dev,)),
            dma((per_dev,)),
            dma((per_dev,)),
            dma((per_dev,)),
            dma((2, max(per_dev, 2))),
            dma((owners,)),
            dma((owners,)),
            dma((owners,)),
            dma((owners,)),
        ],
        compiler_params=pltpu.CompilerParams(
            collective_id=0, has_side_effects=True, vmem_limit_bytes=62 * 2**20
        ),
        name="route",
    )(tok_in, out_grad, gate_weight.transpose(0, 2, 1), up_weight.transpose(0, 2, 1), down_weight)

    batch = 4 if per_dev % 4 == 0 else 1

    def one(a, b):
        return pl.BlockSpec((batch, a, b), lambda e: (e, 0, 0))

    grad_gate, grad_up, grad_down = pl.pallas_call(
        functools.partial(weights_kernel, hid, hid_pad),
        grid=(per_dev // batch,),
        out_shape=(jax.ShapeDtypeStruct(down_weight.shape, BF16),) * 3,
        in_specs=[one(rows, width), one(rows, width), one(rows, 3 * hid_pad)],
        out_specs=(one(hid, width),) * 3,
        compiler_params=pltpu.CompilerParams(vmem_limit_bytes=60 * 2**20),
        name="weight_grads",
    )(xs, gs, back)
    return (
        out[:tok_rows].astype(BF16),
        out[tok_rows : tok_rows + top_count, :tok_rows].T,
        grad_gate.transpose(0, 2, 1),
        grad_up.transpose(0, 2, 1),
        grad_down,
    )


def solution(mesh):
    placed = (
        P(("groups", "expert", "dp"), "inner"),
        P(("groups", "expert", "dp"), "inner"),
        P(("groups", "expert", "dp"), None),
        P(("groups", "expert", "dp"), None),
        P("expert", "inner", "dp"),
        P("expert", "inner", "dp"),
        P("expert", "dp", "inner"),
    )
    return jax.shard_map(
        on_device,
        mesh=mesh,
        in_specs=placed,
        out_specs=(
            P(("groups", "expert", "dp"), "inner"),
            P(("groups", "expert", "dp"), None),
            P(("groups", "expert"), "inner", "dp"),
            P(("groups", "expert"), "inner", "dp"),
            P(("groups", "expert"), "dp", "inner"),
        ),
        check_vma=False,
    )
```
